128 devices in a mesh: row: 16 (over y, z_hi, core), col: 8 (over x, z_lo).
Axes of the slice: x: 4, y: 4, z: 4 (z_hi: 2, z_lo: 2; z = z_hi * 2 + z_lo), core: 2. Of those that a mesh axis runs over, the one named last changes fastest.
Arguments:
- tokens: bfloat16 [6144, 4096], P('row', 'col'), may hold values from -6 to 6
- cotangent: bfloat16 [6144, 4096], P('row', 'col'), may hold values from -6 to 6
- gate_blocks: bfloat16 [32, 32, 128, 128], P('row', 'col'), may hold values from -0.1875 to 0.1875
- up_blocks: bfloat16 [32, 32, 128, 128], P('row', 'col'), may hold values from -0.1875 to 0.1875
- down_blocks: bfloat16 [32, 32, 128, 128], P('row', 'col'), may hold values from -0.09375 to 0.09375
- gate_cols: int32 [32, 32], P('row', 'col'), may hold values from 0 to 127, as said below
- up_cols: int32 [32, 32], P('row', 'col'), may hold values from 0 to 127, as said below
- down_cols: int32 [32, 32], P('row', 'col'), may hold values from 0 to 127, as said below
Outputs:
- output: bfloat16 [6144, 4096], P('row', 'col')
- tokens_grad: bfloat16 [6144, 4096], P('row', 'col')
- gate_grad: bfloat16 [32, 32, 128, 128], P('row', 'col')
- up_grad: bfloat16 [32, 32, 128, 128], P('row', 'col')
- down_grad: bfloat16 [32, 32, 128, 128], P('row', 'col')
The draws below stay inside these ranges and needn't reach their ends.
Inputs may be any that keep to these rules, and one draw needn't show every extreme that they name: In every block row of gate_cols, slots c * 4 to c * 4 + 3 hold 4 different block columns, all in c * 16 to c * 16 + 15. In every block row of up_cols, slots c * 4 to c * 4 + 3 hold 4 different block columns, all in c * 16 to c * 16 + 15. In every block row of down_cols, slots c * 4 to c * 4 + 3 hold 4 different block columns, all in c * 16 to c * 16 + 15.
All inputs are finite; a program needn't handle non-finite values.
Results may differ from the reference program's by a relative error of at most 0.022.
Values may be sent and summed in bfloat16 or wider, within the bound.
No kernel may reach another device: no remote copies, remote signals or barrier semaphores. Data moves between devices by JAX's collectives and lax.ppermute only.
A program may use at most 256 MiB of HBM per device.

```python
import jax
import jax.numpy as jnp
from jax import lax

D = 4096
FF = 16384
B = 128
TOK_DEV = 384
TOKENS = 6144
KB = 32
FB = 128
FB_DEV = 16
NZ = 4
SLOTS = 32
N_ROW = 16


def pattern_draw(key):
    groups = SLOTS // NZ
    row_keys = jax.random.split(key, KB * groups)
    chosen_cols = jax.vmap(lambda subkey: jax.random.permutation(subkey, FB_DEV))(row_keys)[:, :NZ]
    group_start = jnp.arange(KB * groups, dtype=jnp.int32) % groups * FB_DEV
    return (chosen_cols.astype(jnp.int32) + group_start[:, None]).reshape(KB, SLOTS)


def draw_gate_cols(key, part):
    return pattern_draw(jax.random.fold_in(key, 11))


def draw_up_cols(key, part):
    return pattern_draw(jax.random.fold_in(key, 23))


def draw_down_cols(key, part):
    return pattern_draw(jax.random.fold_in(key, 37))


def spiked(values, rng, source, target, blocks, factor):
    owner, partner = [(jnp.arange(values.shape[dim]) // (values.shape[dim] // blocks)).reshape([-1 if axis == dim else 1 for axis in range(values.ndim)]) for dim in (source, target)]
    chosen = jax.random.permutation(rng, blocks)[partner]
    strong = (owner == chosen) | (owner == (partner + blocks // 2) % blocks)
    return jnp.where(strong, factor * values, values)


def levels(stream_key, extent, cuts, smallest, high):
    loudness, own = 1.0, jax.random.fold_in(stream_key, 6)
    for position, blocks in cuts:
        draws = jnp.exp(jax.random.uniform(jax.random.fold_in(own, position), (blocks,), jnp.float32, smallest / len(cuts), high / len(cuts)))
        loudness = loudness * jnp.repeat(draws, extent[position] // blocks).reshape([-1 if axis == position else 1 for axis in range(len(extent))])
    return loudness


def scatter_about(own_key, shape, spread, bound, shards=(), held_as=jnp.bfloat16):
    factor_of = levels(own_key, shape, shards, -0.22, 0.18) if shards else 1.0
    entries = jax.random.normal(own_key, shape, jnp.float32) * spread * factor_of
    return jnp.minimum(jnp.maximum(entries, -bound), bound).astype(held_as)


def heavy_noise(rng, extent, scale, reach, shards, heavy, kind=jnp.bfloat16):
    entries = scale * jax.random.normal(rng, extent, jnp.float32)
    if shards:
        entries = entries * levels(rng, extent, shards, -0.22, 0.18)
    return jnp.clip(spiked(entries, jax.random.fold_in(rng, 3), *heavy), -reach, reach).astype(kind)


def setup_inputs(seed: int = 0) -> dict:
    key_of = jax.random.split(jax.random.key(seed), 9)
    return {
        "tokens": heavy_noise(key_of[0], (TOKENS, D), 1.0, 6.0, ((0, 16), (1, 8)), (0, 1, 16, 2.0)),
        "cotangent": heavy_noise(key_of[1], (TOKENS, D), 1.0, 6.0, ((0, 16), (1, 8)), (0, 1, 16, 2.0)),
        "gate_blocks": scatter_about(key_of[2], (KB, SLOTS, B, B), (D // 4) ** -0.5, 0.1875, ((0, 16), (1, 8))),
        "up_blocks": scatter_about(key_of[3], (KB, SLOTS, B, B), (D // 4) ** -0.5, 0.1875, ((0, 16), (1, 8))),
        "down_blocks": scatter_about(key_of[4], (KB, SLOTS, B, B), (FF // 4) ** -0.5, 0.09375, ((0, 16), (1, 8))),
        "gate_cols": draw_gate_cols(jax.random.fold_in(key_of[8], 71), 0),
        "up_cols": draw_up_cols(jax.random.fold_in(key_of[8], 71), 0),
        "down_cols": draw_down_cols(jax.random.fold_in(key_of[8], 71), 0),
    }


def settle(partial_value):
    rounded = lax.optimization_barrier(partial_value.astype(jnp.bfloat16))
    return rounded.astype(jnp.float32)

def forward_form(inputs, values, columns):

    def advance(running, row_index):
        products = jnp.einsum('td,sde->tse', inputs[:, row_index].astype(jnp.float32), values[row_index].astype(jnp.float32))
        return (running.at[:, columns[row_index]].add(products), None)
    initial = jnp.zeros((TOKENS, FB, B), jnp.float32)
    running, _ = lax.scan(advance, initial, jnp.arange(KB, dtype=jnp.int32))
    return running

def grouped_product(chosen, values):
    groups = SLOTS // NZ
    left_side = chosen.astype(jnp.float32).reshape(TOKENS, groups, NZ, B)
    right_side = values.astype(jnp.float32).reshape(groups, NZ, B, B)
    return jnp.einsum('tcne,cnde->tcd', left_side, right_side)

def reference(tokens, cotangent, gate_blocks, up_blocks, down_blocks, gate_cols, up_cols, down_cols):
    token_blocks = tokens.reshape(TOKENS, KB, B)
    cotangent_blocks = cotangent.reshape(TOKENS, KB, B)
    gate_sums = forward_form(token_blocks, gate_blocks, gate_cols)
    up_sums = forward_form(token_blocks, up_blocks, up_cols)
    hidden = (jax.nn.silu(gate_sums) * up_sums).astype(jnp.bfloat16)

    def output_row(row_index):
        partial_value = grouped_product(hidden[:, down_cols[row_index]], down_blocks[row_index])
        return lax.optimization_barrier(jnp.sum(settle(partial_value), axis=1))
    output = lax.map(output_row, jnp.arange(KB, dtype=jnp.int32))
    output = jnp.transpose(output, (1, 0, 2)).reshape(TOKENS, D).astype(jnp.bfloat16)
    hidden_grad = forward_form(cotangent_blocks, down_blocks, down_cols)
    sigmoid_gate = jax.nn.sigmoid(gate_sums)
    up_delta = (hidden_grad * jax.nn.silu(gate_sums)).astype(jnp.bfloat16)
    gate_delta = (hidden_grad * up_sums * sigmoid_gate * (1.0 + gate_sums * (1.0 - sigmoid_gate))).astype(jnp.bfloat16)

    def input_row(row_index):
        partial_value = grouped_product(gate_delta[:, gate_cols[row_index]], gate_blocks[row_index])
        partial_value = partial_value + grouped_product(up_delta[:, up_cols[row_index]], up_blocks[row_index])
        return lax.optimization_barrier(jnp.sum(settle(partial_value), axis=1))
    tokens_grad = lax.map(input_row, jnp.arange(KB, dtype=jnp.int32))
    tokens_grad = jnp.transpose(tokens_grad, (1, 0, 2)).reshape(TOKENS, D).astype(jnp.bfloat16)
    grad_scale = TOKENS ** (-0.5)

    def weight_row(row_index):
        token_part = token_blocks[:, row_index].astype(jnp.float32).reshape(N_ROW, TOK_DEV, B)
        cotangent_part = cotangent_blocks[:, row_index].astype(jnp.float32).reshape(N_ROW, TOK_DEV, B)

        def block_grad(row_part, deltas, columns):
            chosen = deltas[:, columns[row_index]].astype(jnp.float32).reshape(N_ROW, TOK_DEV, SLOTS, B)
            terms = jnp.einsum('gtd,gtse->gsde', row_part, chosen) * grad_scale
            return lax.optimization_barrier(jnp.sum(settle(terms), axis=0)).astype(jnp.bfloat16)
        return (block_grad(token_part, gate_delta, gate_cols), block_grad(token_part, up_delta, up_cols), block_grad(cotangent_part, hidden, down_cols))
    gate_grad, up_grad, down_grad = lax.map(weight_row, jnp.arange(KB, dtype=jnp.int32))
    return (output, tokens_grad, gate_grad, up_grad, down_grad)
```

```python
import functools

import jax
import jax.numpy as jnp
from jax import lax
from jax.experimental import pallas as pl
from jax.experimental.pallas import tpu as pltpu
from jax.sharding import PartitionSpec as P

BLK = 128
NZ = 4
FB_DEV = 16
X_SIZE = 4
VMEM_BYTES = 56 * 1024 * 1024
NT = (((1,), (1,)), ((), ()))
TN = (((0,), (0,)), ((), ()))


def lanes(values):
    return jnp.concatenate(values, axis=1)


def sums_kernel(order, cols, x_ref, w_ref, hidden_ref, gate_delta_ref, up_delta_ref, acc):
    step = pl.program_id(0)
    tok_rows = hidden_ref.shape[1]

    @pl.when(step == 0)
    def _():
        acc[...] = jnp.zeros_like(acc)

    for i in range(4):
        owner = order[step] * 2 + i // 2
        feat = x_ref[0, :tok_rows, i * BLK : (i + 1) * BLK]
        cot = x_ref[0, tok_rows:, i * BLK : (i + 1) * BLK]
        for t in range(3):
            left = cot if t == 2 else feat
            for pair in range(0, NZ, 2):
                row = (t * 2 + i % 2) * NZ * BLK + pair * BLK
                right = lanes(
                    [w_ref[i // 2, row : row + BLK, :], w_ref[i // 2, row + BLK : row + 2 * BLK, :]]
                )
                prod = jnp.dot(left, right, preferred_element_type=jnp.float32)
                for h in range(2):
                    col = cols[owner * 24 + t * 8 + (i % 2) * NZ + pair + h]
                    acc[t, col] += prod[:, h * BLK : (h + 1) * BLK]

    @pl.when(step == pl.num_programs(0) - 1)
    def _():
        @pl.loop(0, FB_DEV)
        def _(f):
            gate = acc[0, f]
            up = acc[1, f]
            grad = acc[2, f]
            sig = jax.nn.sigmoid(gate)
            silu = gate * sig
            hidden_ref[f] = (silu * up).astype(jnp.bfloat16)
            up_delta_ref[f] = (grad * silu).astype(jnp.bfloat16)
            gate_delta_ref[f] = (grad * up * sig * (1.0 + gate * (1.0 - sig))).astype(jnp.bfloat16)


def weight_grads_kernel(scale, order, cols, x_ref, hidden_ref, gate_delta_ref, up_delta_ref, o_ref):
    step = pl.program_id(0)
    tok_rows = hidden_ref.shape[1]
    for i in range(4):
        owner = order[step] * 2 + i // 2
        feat = x_ref[0, :tok_rows, i * BLK : (i + 1) * BLK]
        cot = x_ref[0, tok_rows:, i * BLK : (i + 1) * BLK]
        for t, source in enumerate((gate_delta_ref, up_delta_ref, hidden_ref)):
            left = cot if t == 2 else feat
            base = owner * 24 + t * 8 + (i % 2) * NZ
            right = lanes([source[cols[base + s]] for s in range(NZ)])
            prod = lax.dot_general(left, right, TN, preferred_element_type=jnp.float32) * scale
            row = (t * 2 + i % 2) * NZ * BLK
            for s in range(NZ):
                o_ref[i // 2, row + s * BLK : row + (s + 1) * BLK, :] = prod[
                    :, s * BLK : (s + 1) * BLK
                ].astype(jnp.bfloat16)


def product_kernel(tensors, cols, w_ref, *refs):
    step = pl.program_id(0)
    sources, o_ref = refs[:-1], refs[-1]
    for i in range(4):
        owner = step * 2 + i // 2
        left, right = [], []
        for n, t in enumerate(tensors):
            base = owner * 24 + t * 8 + (i % 2) * NZ
            row = (n * 2 + i % 2) * NZ * BLK
            for s in range(NZ):
                left.append(sources[n][cols[base + s]])
                right.append(w_ref[i // 2, row + s * BLK : row + (s + 1) * BLK, :])
        prod = lax.dot_general(lanes(left), lanes(right), NT, preferred_element_type=jnp.float32)
        o_ref[0, :, i * BLK : (i + 1) * BLK] = prod.astype(jnp.bfloat16)


def cost(flops, moved):
    return pl.CostEstimate(flops=flops, bytes_accessed=moved, transcendentals=0)


def params():
    return pltpu.CompilerParams(
        dimension_semantics=("arbitrary",), vmem_limit_bytes=VMEM_BYTES
    )


def whole(shape):
    return pl.BlockSpec(shape, lambda j, *_: (0,) * len(shape))


def local_sums(order, cols, feats, weights):
    steps, rows2, width = feats.shape
    tok_rows = rows2 // 2
    shape = (FB_DEV, tok_rows, BLK)
    per = weights.shape[1]
    out = jax.ShapeDtypeStruct(shape, jnp.bfloat16)
    return pl.pallas_call(
        sums_kernel,
        out_shape=(out, out, out),
        grid_spec=pltpu.PrefetchScalarGridSpec(
            num_scalar_prefetch=2,
            grid=(steps,),
            in_specs=[
                pl.BlockSpec((1, rows2, width), lambda j, order, cols: (j, 0, 0)),
                pl.BlockSpec((2, per, BLK), lambda j, order, cols: (order[j], 0, 0)),
            ],
            out_specs=[whole(shape)] * 3,
            scratch_shapes=[pltpu.VMEM((3,) + shape, jnp.float32)],
        ),
        compiler_params=params(),
        cost_estimate=cost(10**10, 30 * 10**6),
        name="local_sums",
    )(order, cols, feats, weights)


def weight_grads(order, cols, feats, hidden, gate_delta, up_delta, scale):
    steps, rows2, width = feats.shape
    rows = 3 * 2 * NZ * BLK
    return pl.pallas_call(
        functools.partial(weight_grads_kernel, scale),
        out_shape=jax.ShapeDtypeStruct((2 * steps, rows, BLK), jnp.bfloat16),
        grid_spec=pltpu.PrefetchScalarGridSpec(
            num_scalar_prefetch=2,
            grid=(steps,),
            in_specs=[pl.BlockSpec((1, rows2, width), lambda j, order, cols: (j, 0, 0))]
            + [whole(hidden.shape)] * 3,
            out_specs=pl.BlockSpec((2, rows, BLK), lambda j, order, cols: (order[j], 0, 0)),
        ),
        compiler_params=params(),
        cost_estimate=cost(10**10, 25 * 10**6),
        name="weight_grads",
    )(order, cols, feats, hidden, gate_delta, up_delta)


def block_product(tensors, cols, weights, sources):
    tok_rows = sources[0].shape[1]
    steps = weights.shape[0] // 2
    rows = len(tensors) * 2 * NZ * BLK
    at = tensors[0] * 2 * NZ * BLK // rows
    return pl.pallas_call(
        functools.partial(product_kernel, tensors),
        out_shape=jax.ShapeDtypeStruct((steps, tok_rows, 4 * BLK), jnp.bfloat16),
        grid_spec=pltpu.PrefetchScalarGridSpec(
            num_scalar_prefetch=1,
            grid=(steps,),
            in_specs=[pl.BlockSpec((2, rows, BLK), lambda j, cols: (j, at, 0))]
            + [whole(sources[0].shape)] * len(sources),
            out_specs=pl.BlockSpec((1, tok_rows, 4 * BLK), lambda j, cols: (j, 0, 0)),
        ),
        compiler_params=params(),
        cost_estimate=cost(len(tensors) * 3 * 10**9, len(tensors) * 7 * 10**6),
        name="block_product",
    )(cols, weights, *sources)


def over_x(value, shift, cols):
    pairs = [(c, ((c // 2 + shift) % X_SIZE) * 2 + c % 2) for c in range(cols)]
    return lax.ppermute(value, "col", pairs)


def gather_features(own, cols):
    me = lax.axis_index("col")
    x, z = me // 2, me % 2
    near = lax.ppermute(own, "col", [(c, c ^ 1) for c in range(cols)])
    own_w, own_e = over_x(own, 1, cols), over_x(own, -1, cols)
    near_w, near_e = over_x(near, 1, cols), over_x(near, -1, cols)
    own_far, near_far = over_x(own_w, 1, cols), over_x(near_e, -1, cols)
    pieces = [own, near, own_w, own_e, near_w, near_e, own_far, near_far]
    shifts = [(0, 0), (0, 1), (-1, 0), (1, 0), (-1, 1), (1, 1), (2, 0), (2, 1)]
    order = [((x + dx) % X_SIZE) * 2 + (z + dz) % 2 for dx, dz in shifts]
    return jnp.stack(pieces), jnp.stack(order).astype(jnp.int32)


def body(tokens, cotangent, gate_blocks, up_blocks, down_blocks, gate_cols, up_cols, down_cols):
    n_row, n_col = lax.axis_size("row"), lax.axis_size("col")
    tok_rows = tokens.shape[0]
    tables = jnp.concatenate(
        [jnp.bitwise_and(t, FB_DEV - 1).reshape(1, -1) for t in (gate_cols, up_cols, down_cols)], 1
    ).astype(jnp.bfloat16)
    tables = jnp.pad(tables, ((0, 15), (0, BLK - tables.shape[1])))
    packed = jnp.concatenate(
        [b.reshape(-1, BLK) for b in (gate_blocks, up_blocks, down_blocks)] + [tables], 0
    )
    weights = lax.all_gather(packed, "row", axis=0, tiled=True).reshape(n_row, -1, BLK)
    feats, order = gather_features(jnp.concatenate([tokens, cotangent], 0), n_col)
    at = packed.shape[0] - 16
    cols = weights[:, at, : 3 * 2 * NZ].astype(jnp.int32).reshape(-1)
    hidden, gate_delta, up_delta = local_sums(order, cols, feats, weights)
    scale = float(tok_rows * n_row) ** (-0.5)
    terms = weight_grads(order, cols, feats, hidden, gate_delta, up_delta, scale)
    grads = lax.psum_scatter(terms.reshape(-1, BLK), "row", scatter_dimension=0, tiled=True)
    gate_grad, up_grad, down_grad = (
        g.reshape(gate_blocks.shape) for g in jnp.split(grads, 3, axis=0)
    )

    def reduce_features(partial_value):
        parts = lax.all_to_all(partial_value, "col", 0, 0, tiled=True)
        return jnp.sum(parts.astype(jnp.float32), axis=0).astype(jnp.bfloat16)

    output = reduce_features(block_product((2,), cols, weights, (hidden,)))
    tokens_grad = reduce_features(block_product((0, 1), cols, weights, (gate_delta, up_delta)))
    return (output, tokens_grad, gate_grad, up_grad, down_grad)


def solution(mesh):
    flat, blocks = P("row", "col"), P("row", "col", None, None)
    in_specs = (flat, flat, blocks, blocks, blocks, flat, flat, flat)
    out_specs = (flat, flat, blocks, blocks, blocks)
    return jax.shard_map(body, mesh=mesh, in_specs=in_specs, out_specs=out_specs, check_vma=False)
```

```python
import functools

import jax
import jax.numpy as jnp
from jax import lax
from jax.experimental import pallas as pl
from jax.experimental.pallas import tpu as pltpu
from jax.sharding import PartitionSpec as P

BLK = 128
NZ = 4
FB_DEV = 16
RING = 4
VMEM_BYTES = 56 * 1024 * 1024
NT = (((1,), (1,)), ((), ()))
TN = (((0,), (0,)), ((), ()))


def lanes(values):
    return jnp.concatenate(values, axis=1)


def read_piece(sources, slots, held, sems):
    return [
        pltpu.make_async_copy(source, held.at[slot], sems.at[n])
        for n, (source, slot) in enumerate(zip(sources, slots))
    ]


def sums_kernel(n_feat, n_w, chips, owners, cols, *refs):
    feats, weights = refs[:n_feat], refs[n_feat : n_feat + n_w]
    hidden_ref, gate_delta_ref, up_delta_ref = refs[n_feat + n_w : n_feat + n_w + 3]
    acc, held_x, held_w, sem_x, sem_w = refs[n_feat + n_w + 3 :]
    tok_rows = hidden_ref.shape[1]
    copies_x = read_piece(feats, [chips[n] for n in range(n_feat)], held_x, sem_x)
    copies_w = read_piece(weights, range(n_w), held_w, sem_w)
    for copy in copies_x + copies_w:
        copy.start()
    acc[...] = jnp.zeros_like(acc)
    for copy in copies_x:
        copy.wait()

    def piece(p, carry):
        pltpu.make_async_copy(weights[0], held_w.at[p], sem_w.at[p]).wait()
        owner = owners[p]
        for i in range(2):
            at = pl.ds(pl.multiple_of((owner % 2) * 2 * BLK + i * BLK, BLK), BLK)
            feat = held_x[owner // 2, :tok_rows, at]
            cot = held_x[owner // 2, tok_rows:, at]
            for t in range(3):
                left = cot if t == 2 else feat
                for pair in range(0, NZ, 2):
                    row = (t * 2 + i) * NZ * BLK + pair * BLK
                    right = lanes(
                        [held_w[p, row : row + BLK, :], held_w[p, row + BLK : row + 2 * BLK, :]]
                    )
                    prod = jnp.dot(left, right, preferred_element_type=jnp.float32)
                    for h in range(2):
                        col = cols[p * 24 + t * 8 + i * NZ + pair + h]
                        acc[t, col] += prod[:, h * BLK : (h + 1) * BLK]
        return carry

    lax.fori_loop(0, n_w, piece, 0)

    @pl.loop(0, FB_DEV)
    def _(f):
        gate = acc[0, f]
        up = acc[1, f]
        grad = acc[2, f]
        sig = jax.nn.sigmoid(gate)
        silu = gate * sig
        hidden_ref[f] = (silu * up).astype(jnp.bfloat16)
        up_delta_ref[f] = (grad * silu).astype(jnp.bfloat16)
        gate_delta_ref[f] = (grad * up * sig * (1.0 + gate * (1.0 - sig))).astype(jnp.bfloat16)


def weight_grads_kernel(n_feat, tensors, half, scale, chips, owners, cols, *refs):
    feats, sources = refs[:n_feat], refs[n_feat : n_feat + len(tensors)]
    o_ref, held_x, sem_x = refs[n_feat + len(tensors) :]
    tok_rows = held_x.shape[1]
    first = tok_rows if tensors[0] == 2 else 0
    copies = read_piece(
        [f.at[pl.ds(first, tok_rows)] for f in feats], [chips[n] for n in range(n_feat)], held_x, sem_x
    )
    for copy in copies:
        copy.start()
    for copy in copies:
        copy.wait()

    def slot(p, carry):
        owner = owners[half * 8 + p]
        for i in range(2):
            at = pl.ds(pl.multiple_of((owner % 2) * 2 * BLK + i * BLK, BLK), BLK)
            left = held_x[owner // 2, :, at]
            right = []
            for n, t in enumerate(tensors):
                base = (half * 8 + p) * 24 + t * 8 + i * NZ
                right += [sources[n][cols[base + s]] for s in range(NZ)]
            prod = lax.dot_general(left, lanes(right), TN, preferred_element_type=jnp.float32) * scale
            for n in range(len(tensors)):
                for s in range(NZ):
                    row = (n * 2 + i) * NZ * BLK + s * BLK
                    at_col = (n * NZ + s) * BLK
                    o_ref[p, row : row + BLK, :] = prod[:, at_col : at_col + BLK].astype(jnp.bfloat16)
        return carry

    lax.fori_loop(0, 8, slot, 0)


def product_kernel(n_w, tensors, owners, cols, *refs):
    weights, sources = refs[:n_w], refs[n_w : n_w + len(tensors)]
    o_ref, held_w, sem_w = refs[n_w + len(tensors) :]
    rows = held_w.shape[1]
    views = [w.at[pl.ds(tensors[0] * 2 * NZ * BLK, rows)] for w in weights]
    for copy in read_piece(views, range(n_w), held_w, sem_w):
        copy.start()

    def piece(p, carry):
        pltpu.make_async_copy(views[0], held_w.at[p], sem_w.at[p]).wait()
        owner = owners[p]
        for i in range(2):
            left, right = [], []
            for n, t in enumerate(tensors):
                base = p * 24 + t * 8 + i * NZ
                row = (n * 2 + i) * NZ * BLK
                for s in range(NZ):
                    left.append(sources[n][cols[base + s]])
                    right.append(held_w[p, row + s * BLK : row + (s + 1) * BLK, :])
            prod = lax.dot_general(lanes(left), lanes(right), NT, preferred_element_type=jnp.float32)
            at = pl.ds(pl.multiple_of((owner % 2) * 2 * BLK + i * BLK, BLK), BLK)
            o_ref[owner // 2, :, at] = prod.astype(jnp.bfloat16)
        return carry

    lax.fori_loop(0, n_w, piece, 0)


def cost(flops, moved):
    return pl.CostEstimate(flops=flops, bytes_accessed=moved, transcendentals=0)


PARAMS = pltpu.CompilerParams(vmem_limit_bytes=VMEM_BYTES)
SMEM = pl.BlockSpec(memory_space=pltpu.SMEM)
VMEM = pl.BlockSpec(memory_space=pltpu.VMEM)
ANY = pl.BlockSpec(memory_space=pl.ANY)


def local_sums(chips, owners, cols, feats, weights):
    rows2, width = feats[0].shape
    shape = (FB_DEV, rows2 // 2, BLK)
    out = jax.ShapeDtypeStruct(shape, jnp.bfloat16)
    return pl.pallas_call(
        functools.partial(sums_kernel, len(feats), len(weights)),
        out_shape=(out, out, out),
        in_specs=[SMEM] * 3 + [ANY] * (len(feats) + len(weights)),
        out_specs=(VMEM, VMEM, VMEM),
        scratch_shapes=[
            pltpu.VMEM((3,) + shape, jnp.float32),
            pltpu.VMEM((len(feats), rows2, width), jnp.bfloat16),
            pltpu.VMEM((len(weights),) + weights[0].shape, jnp.bfloat16),
            pltpu.SemaphoreType.DMA((len(feats),)),
            pltpu.SemaphoreType.DMA((len(weights),)),
        ],
        compiler_params=PARAMS,
        cost_estimate=cost(10**10, 30 * 10**6),
        name="local_sums",
    )(chips, owners, cols, *feats, *weights)


def weight_grads(tensors, half, chips, owners, cols, feats, sources, scale):
    rows2, width = feats[0].shape
    rows = len(tensors) * 2 * NZ * BLK
    return pl.pallas_call(
        functools.partial(weight_grads_kernel, len(feats), tensors, half, scale),
        out_shape=jax.ShapeDtypeStruct((8, rows, BLK), jnp.bfloat16),
        in_specs=[SMEM] * 3 + [ANY] * len(feats) + [VMEM] * len(sources),
        out_specs=VMEM,
        scratch_shapes=[
            pltpu.VMEM((len(feats), rows2 // 2, width), jnp.bfloat16),
            pltpu.SemaphoreType.DMA((len(feats),)),
        ],
        compiler_params=PARAMS,
        cost_estimate=cost(len(tensors) * 2 * 10**9, len(tensors) * 6 * 10**6),
        name="weight_grads",
    )(chips, owners, cols, *feats, *sources)


def block_product(tensors, owners, cols, weights, sources):
    tok_rows = sources[0].shape[1]
    rows = len(tensors) * 2 * NZ * BLK
    return pl.pallas_call(
        functools.partial(product_kernel, len(weights), tensors),
        out_shape=jax.ShapeDtypeStruct((len(weights) // 2, tok_rows, 4 * BLK), jnp.bfloat16),
        in_specs=[SMEM] * 2 + [ANY] * len(weights) + [VMEM] * len(sources),
        out_specs=VMEM,
        scratch_shapes=[
            pltpu.VMEM((len(weights), rows, BLK), jnp.bfloat16),
            pltpu.SemaphoreType.DMA((len(weights),)),
        ],
        compiler_params=PARAMS,
        cost_estimate=cost(len(tensors) * 3 * 10**9, len(tensors) * 7 * 10**6),
        name="block_product",
    )(owners, cols, *weights, *sources)


SHIFTS = ((0, 0), (0, 1), (-1, 0), (1, 0), (-1, 1), (1, 1), (2, 0), (2, 1))


def permute(value, axis, target):
    return lax.ppermute(value, axis, [(i, target(i)) for i in range(lax.axis_size(axis))])


def over_x(value, shift):
    return permute(value, "col", lambda c: ((c // 2 + shift) % RING) * 2 + c % 2)


def over_y(value, shift):
    return permute(value, "row", lambda r: ((r // 4 + shift) % RING) * 4 + r % 4)


def ring_gather(own, near, ring):
    own_m, own_p = ring(own, 1), ring(own, -1)
    near_m, near_p = ring(near, 1), ring(near, -1)
    return [own, near, own_m, own_p, near_m, near_p, ring(own_m, 1), ring(near_p, -1)]


def gather_features(own):
    near = permute(own, "col", lambda c: c ^ 1)
    me = lax.axis_index("col")
    chips = [((me // 2 + d) % RING) * 2 + (me % 2 + e) % 2 for d, e in SHIFTS]
    return ring_gather(own, near, over_x), jnp.stack(chips).astype(jnp.int32)


def other_core(value):
    return permute(value, "row", lambda r: r ^ 1)


def gather_weights(own):
    near = permute(own, "row", lambda r: r ^ 2)
    same = ring_gather(own, near, over_y)
    me = lax.axis_index("row")
    chip = me // 2
    chips = [((chip // 2 + d) % RING) * 2 + (chip % 2 + e) % 2 for d, e in SHIFTS]
    owners = [c * 2 + me % 2 for c in chips]
    owners += [c * 2 + 1 - me % 2 for c in chips]
    return same + [other_core(p) for p in same], jnp.stack(owners).astype(jnp.int32)


def reduce_slots(mine, theirs):
    got = other_core(theirs)

    def slot(k):
        return mine[k].astype(jnp.float32) + got[k].astype(jnp.float32)

    def wire(*values):
        return jnp.concatenate([v.astype(jnp.bfloat16) for v in values], 0)

    far_p = over_y(wire(slot(6)), 1).astype(jnp.float32)
    far_m = over_y(wire(slot(7)), -1).astype(jnp.float32)
    from_m = over_y(wire(slot(3) + far_p, slot(5)), 1).astype(jnp.float32)
    from_p = over_y(wire(slot(2), slot(4) + far_m), -1).astype(jnp.float32)
    rows = mine.shape[1]
    keep = slot(0) + from_m[:rows] + from_p[:rows]
    give = slot(1) + from_m[rows:] + from_p[rows:]
    last = permute(wire(give), "row", lambda r: r ^ 2)
    return (keep + last.astype(jnp.float32)).astype(jnp.bfloat16)


def body(tokens, cotangent, gate_blocks, up_blocks, down_blocks, gate_cols, up_cols, down_cols):
    tok_rows = tokens.shape[0]
    tables = jnp.concatenate(
        [jnp.bitwise_and(t, FB_DEV - 1).reshape(1, -1) for t in (gate_cols, up_cols, down_cols)], 1
    ).astype(jnp.bfloat16)
    tables = jnp.pad(tables, ((0, 15), (0, BLK - tables.shape[1])))
    packed = jnp.concatenate(
        [b.reshape(-1, BLK) for b in (gate_blocks, up_blocks, down_blocks)] + [tables], 0
    )
    at = packed.shape[0] - 16
    weights, owners = gather_weights(packed)
    feats, chips = gather_features(jnp.concatenate([tokens, cotangent], 0))
    cols = jnp.concatenate([w[at, : 3 * 2 * NZ] for w in weights]).astype(jnp.int32)
    hidden, gate_delta, up_delta = local_sums(chips, owners, cols, feats, weights)
    scale = float(tok_rows * lax.axis_size("row")) ** (-0.5)

    def grads(tensors, sources):
        theirs = weight_grads(tensors, 1, chips, owners, cols, feats, sources, scale)
        mine = weight_grads(tensors, 0, chips, owners, cols, feats, sources, scale)
        return reduce_slots(mine, theirs)

    def reduce_features(partial_value):
        parts = lax.all_to_all(partial_value, "col", 0, 0, tiled=True)
        return jnp.sum(parts.astype(jnp.float32), axis=0).astype(jnp.bfloat16)

    down_grad = grads((2,), (hidden,)).reshape(down_blocks.shape)
    output = reduce_features(block_product((2,), owners, cols, weights, (hidden,)))
    both = grads((0, 1), (gate_delta, up_delta))
    gate_grad, up_grad = (g.reshape(gate_blocks.shape) for g in jnp.split(both, 2, axis=0))
    tokens_grad = reduce_features(
        block_product((0, 1), owners, cols, weights, (gate_delta, up_delta))
    )
    return (output, tokens_grad, gate_grad, up_grad, down_grad)


def solution(mesh):
    flat, blocks = P("row", "col"), P("row", "col", None, None)
    in_specs = (flat, flat, blocks, blocks, blocks, flat, flat, flat)
    out_specs = (flat, flat, blocks, blocks, blocks)
    return jax.shard_map(body, mesh=mesh, in_specs=in_specs, out_specs=out_specs, check_vma=False)
```

```python
import functools

import jax
import jax.numpy as jnp
from jax import lax
from jax.experimental import pallas as pl
from jax.experimental.pallas import tpu as pltpu
from jax.sharding import PartitionSpec as P

BLK = 128
NZ = 4
FB_DEV = 16
RING = 4
NT = (((1,), (1,)), ((), ()))
TN = (((0,), (0,)), ((), ()))


def lanes(values):
    return jnp.concatenate(values, axis=1)


def sums_kernel(order, cols, x_ref, w_ref, hidden_ref, gate_delta_ref, up_delta_ref, acc):
    step = pl.program_id(0)
    tok_rows = hidden_ref.shape[1]

    @pl.when(step == 0)
    def _():
        acc[...] = jnp.zeros_like(acc)

    for i in range(4):
        owner = order[step] * 2 + i // 2
        feat = x_ref[0, :tok_rows, i * BLK : (i + 1) * BLK]
        cot = x_ref[0, tok_rows:, i * BLK : (i + 1) * BLK]
        for t in range(3):
            left = cot if t == 2 else feat
            for pair in range(0, NZ, 2):
                row = (t * 2 + i % 2) * NZ * BLK + pair * BLK
                right = lanes(
                    [w_ref[i // 2, row : row + BLK, :], w_ref[i // 2, row + BLK : row + 2 * BLK, :]]
                )
                prod = jnp.dot(left, right, preferred_element_type=jnp.float32)
                for h in range(2):
                    col = cols[owner * 24 + t * 8 + (i % 2) * NZ + pair + h]
                    acc[t, col] += prod[:, h * BLK : (h + 1) * BLK]

    @pl.when(step == pl.num_programs(0) - 1)
    def _():
        @pl.loop(0, FB_DEV)
        def _(f):
            gate = acc[0, f]
            up = acc[1, f]
            grad = acc[2, f]
            sig = jax.nn.sigmoid(gate)
            silu = gate * sig
            hidden_ref[f] = (silu * up).astype(jnp.bfloat16)
            up_delta_ref[f] = (grad * silu).astype(jnp.bfloat16)
            gate_delta_ref[f] = (grad * up * sig * (1.0 + gate * (1.0 - sig))).astype(jnp.bfloat16)


def weight_grads_kernel(scale, count, at_x, owners, cols, x_ref, *refs):
    hidden_ref, gate_delta_ref, up_delta_ref = refs[:3]
    step = pl.program_id(0)
    owner = owners[step]
    tok_rows = hidden_ref.shape[1]
    for i in range(2):
        at = pl.ds(pl.multiple_of((owner % 2) * 2 * BLK + i * BLK, BLK), BLK)
        feat = x_ref[0, :tok_rows, at]
        cot = x_ref[0, tok_rows:, at]
        for t, source in enumerate((gate_delta_ref, up_delta_ref, hidden_ref)):
            left = cot if t == 2 else feat
            base = owner * 24 + t * 8 + i * NZ
            right = lanes([source[cols[base + s]] for s in range(NZ)])
            prod = lax.dot_general(left, right, TN, preferred_element_type=jnp.float32) * scale
            for s in range(NZ):
                row = (t * 2 + i) * NZ * BLK + s * BLK
                value = prod[:, s * BLK : (s + 1) * BLK]
                if count:
                    got = refs[3][0, row : row + BLK, :].astype(jnp.float32)
                    value = value + got
                    held = refs[4 + count]
                    held[step, row : row + BLK, :] = value.astype(jnp.bfloat16)
                else:
                    refs[-1][0, row : row + BLK, :] = value.astype(jnp.bfloat16)
    if count:
        outs, held, sems = refs[4 : 4 + count], refs[4 + count], refs[5 + count]
        for n in range(count):

            @pl.when(step == n)
            def _():
                pltpu.make_async_copy(held.at[n], outs[n], sems.at[n]).start()

        @pl.when(step == count - 1)
        def _():
            for n in range(count):
                pltpu.make_async_copy(held.at[n], outs[n], sems.at[n]).wait()


def product_kernel(tensors, cols, w_ref, *refs):
    step = pl.program_id(0)
    sources, o_ref = refs[:-1], refs[-1]
    for i in range(4):
        owner = step * 2 + i // 2
        left, right = [], []
        for n, t in enumerate(tensors):
            base = owner * 24 + t * 8 + (i % 2) * NZ
            row = (n * 2 + i % 2) * NZ * BLK
            for s in range(NZ):
                left.append(sources[n][cols[base + s]])
                right.append(w_ref[i // 2, row + s * BLK : row + (s + 1) * BLK, :])
        prod = lax.dot_general(lanes(left), lanes(right), NT, preferred_element_type=jnp.float32)
        o_ref[0, :, i * BLK : (i + 1) * BLK] = prod.astype(jnp.bfloat16)


def cost(flops, moved):
    return pl.CostEstimate(flops=flops, bytes_accessed=moved, transcendentals=0)


def params(megabytes):
    return pltpu.CompilerParams(
        dimension_semantics=("arbitrary",), vmem_limit_bytes=megabytes * 1024 * 1024
    )


def whole(shape):
    return pl.BlockSpec(shape, lambda j, *_: (0,) * len(shape))


def local_sums(order, cols, feats, weights):
    steps, rows2, width = feats.shape
    tok_rows = rows2 // 2
    shape = (FB_DEV, tok_rows, BLK)
    per = weights.shape[1]
    out = jax.ShapeDtypeStruct(shape, jnp.bfloat16)
    return pl.pallas_call(
        sums_kernel,
        out_shape=(out, out, out),
        grid_spec=pltpu.PrefetchScalarGridSpec(
            num_scalar_prefetch=2,
            grid=(steps,),
            in_specs=[
                pl.BlockSpec((1, rows2, width), lambda j, order, cols: (j, 0, 0)),
                pl.BlockSpec((2, per, BLK), lambda j, order, cols: (order[j], 0, 0)),
            ],
            out_specs=[whole(shape)] * 3,
            scratch_shapes=[pltpu.VMEM((3,) + shape, jnp.float32)],
        ),
        compiler_params=params(56),
        cost_estimate=cost(10**10, 30 * 10**6),
        name="local_sums",
    )(order, cols, feats, weights)


def weight_grads(at_x, owners, cols, feats, sources, scale, got=None):
    _, rows2, width = feats.shape
    count = owners.shape[0]
    rows = 3 * 2 * NZ * BLK
    block = pl.BlockSpec((1, rows, BLK), lambda j, *_: (j, 0, 0))
    in_specs = [pl.BlockSpec((1, rows2, width), lambda j, at_x, *_: (at_x[j], 0, 0))]
    in_specs += [pl.BlockSpec(memory_space=pltpu.VMEM)] * 3
    if got is None:
        out_shape = jax.ShapeDtypeStruct((count, rows, BLK), jnp.bfloat16)
        out_specs, scratch, extra = block, [], ()
    else:
        in_specs.append(block)
        out_shape = (jax.ShapeDtypeStruct((rows, BLK), jnp.bfloat16),) * count
        out_specs = (pl.BlockSpec(memory_space=pl.ANY),) * count
        scratch = [
            pltpu.VMEM((count, rows, BLK), jnp.bfloat16),
            pltpu.SemaphoreType.DMA((count,)),
        ]
        extra = (got,)
    return pl.pallas_call(
        functools.partial(weight_grads_kernel, scale, 0 if got is None else count),
        out_shape=out_shape,
        grid_spec=pltpu.PrefetchScalarGridSpec(
            num_scalar_prefetch=3,
            grid=(count,),
            in_specs=in_specs,
            out_specs=out_specs,
            scratch_shapes=scratch,
        ),
        compiler_params=params(28),
        cost_estimate=cost(count * 10**9, count * 3 * 10**6),
        name="weight_grads",
    )(at_x, owners, cols, feats, *sources, *extra)


def block_product(tensors, cols, weights, sources):
    tok_rows = sources[0].shape[1]
    steps = weights.shape[0] // 2
    rows = len(tensors) * 2 * NZ * BLK
    at = tensors[0] * 2 * NZ * BLK // rows
    return pl.pallas_call(
        functools.partial(product_kernel, tensors),
        out_shape=jax.ShapeDtypeStruct((steps, tok_rows, 4 * BLK), jnp.bfloat16),
        grid_spec=pltpu.PrefetchScalarGridSpec(
            num_scalar_prefetch=1,
            grid=(steps,),
            in_specs=[pl.BlockSpec((2, rows, BLK), lambda j, cols: (j, at, 0))]
            + [whole(sources[0].shape)] * len(sources),
            out_specs=pl.BlockSpec((1, tok_rows, 4 * BLK), lambda j, cols: (j, 0, 0)),
        ),
        compiler_params=params(40),
        cost_estimate=cost(len(tensors) * 3 * 10**9, len(tensors) * 7 * 10**6),
        name="block_product",
    )(cols, weights, *sources)


def permute(value, axis, target):
    return lax.ppermute(value, axis, [(i, target(i)) for i in range(lax.axis_size(axis))])


def over_x(value, shift):
    return permute(value, "col", lambda c: ((c // 2 + shift) % RING) * 2 + c % 2)


def over_y(value, shift):
    return permute(value, "row", lambda r: ((r // 4 + shift) % RING) * 4 + r % 4)


def gather_features(own):
    x, z = lax.axis_index("col") // 2, lax.axis_index("col") % 2
    near = permute(own, "col", lambda c: c ^ 1)
    own_m, own_p = over_x(own, 1), over_x(own, -1)
    near_m, near_p = over_x(near, 1), over_x(near, -1)
    own_far, near_far = over_x(own_m, 1), over_x(near_p, -1)
    pieces = [own, near, own_p, near_p, own_far, near_far, own_m, near_m]
    order = [((x + n // 2) % RING) * 2 + (z + n) % 2 for n in range(8)]
    return jnp.stack(pieces), jnp.stack(order).astype(jnp.int32)


def slot_tables(shifts, half):
    x, z = lax.axis_index("col") // 2, lax.axis_index("col") % 2
    row = lax.axis_index("row")
    chips = [((row // 4 + d) % RING, (row // 2 + e) % 2) for d, e in shifts]
    at_x = [((y - x) % RING) * 2 + (h - z) % 2 for y, h in chips]
    owners = [y * 4 + h * 2 + (row + half) % 2 for y, h in chips]
    return jnp.stack(at_x).astype(jnp.int32), jnp.stack(owners).astype(jnp.int32)


FAR = ((2, 0), (2, 1))
NEAR = ((1, 1), (-1, 1), (1, 0), (-1, 0))
OWN = ((0, 0), (0, 1))


def body(tokens, cotangent, gate_blocks, up_blocks, down_blocks, gate_cols, up_cols, down_cols):
    n_row = lax.axis_size("row")
    tok_rows = tokens.shape[0]
    tables = jnp.concatenate(
        [jnp.bitwise_and(t, FB_DEV - 1).reshape(1, -1) for t in (gate_cols, up_cols, down_cols)], 1
    ).astype(jnp.bfloat16)
    tables = jnp.pad(tables, ((0, 15), (0, BLK - tables.shape[1])))
    packed = jnp.concatenate(
        [b.reshape(-1, BLK) for b in (gate_blocks, up_blocks, down_blocks)] + [tables], 0
    )
    weights = lax.all_gather(packed, "row", axis=0, tiled=True).reshape(n_row, -1, BLK)
    feats, order = gather_features(jnp.concatenate([tokens, cotangent], 0))
    at = packed.shape[0] - 16
    cols = weights[:, at, : 3 * 2 * NZ].astype(jnp.int32).reshape(-1)
    hidden, gate_delta, up_delta = local_sums(order, cols, feats, weights)
    sources = (hidden, gate_delta, up_delta)
    scale = float(tok_rows * n_row) ** (-0.5)

    def after(value):
        return lax.optimization_barrier((cols, value))[0]

    def theirs(shifts, cols):
        return weight_grads(*slot_tables(shifts, 1), cols, feats, sources, scale)

    def mine(shifts, cols, got):
        return weight_grads(*slot_tables(shifts, 0), cols, feats, sources, scale, got)

    def other_core(value):
        return permute(value, "row", lambda r: r ^ 1)

    def reduce_features(partial_value):
        parts = lax.all_to_all(partial_value, "col", 0, 0, tiled=True)
        return jnp.sum(parts.astype(jnp.float32), axis=0).astype(jnp.bfloat16)

    def total(*values):
        return sum(v.astype(jnp.float32) for v in values).astype(jnp.bfloat16)

    out_parts = block_product((2,), cols, weights, (hidden,))
    output = reduce_features(out_parts)
    their_far = theirs(FAR, after(out_parts))
    got_far = other_core(their_far)
    their_near = theirs(NEAR, after(their_far))
    got_near = other_core(their_near)
    far0, far1 = mine(FAR, after(their_near), got_far)
    far_p, far_m = over_y(far0, 1), over_y(far1, -1)
    in_parts = block_product((0, 1), after(far0), weights, (gate_delta, up_delta))
    tokens_grad = reduce_features(in_parts)
    their_own = theirs(OWN, after(in_parts))
    got_own = other_core(their_own)
    p1, m1, p0, m0 = mine(NEAR, after(their_own), got_near)
    from_m1, from_p1 = over_y(p1, 1), over_y(total(m1, far_m), -1)
    from_m0, from_p0 = over_y(total(p0, far_p), 1), over_y(m0, -1)
    own0, own1 = mine(OWN, after(p1), got_own)
    last = permute(total(own1, from_m1, from_p1), "row", lambda r: r ^ 2)
    grads = total(own0, from_m0, from_p0, last)
    gate_grad, up_grad, down_grad = (
        g.reshape(gate_blocks.shape) for g in jnp.split(grads, 3, axis=0)
    )
    return (output, tokens_grad, gate_grad, up_grad, down_grad)


def solution(mesh):
    flat, blocks = P("row", "col"), P("row", "col", None, None)
    in_specs = (flat, flat, blocks, blocks, blocks, flat, flat, flat)
    out_specs = (flat, flat, blocks, blocks, blocks)
    return jax.shard_map(body, mesh=mesh, in_specs=in_specs, out_specs=out_specs, check_vma=False)
```

```python
import functools

import jax
import jax.numpy as jnp
from jax import lax
from jax.experimental import pallas as pl
from jax.experimental.pallas import tpu as pltpu
from jax.sharding import PartitionSpec as P

BLK = 128
NZ = 4
FB_DEV = 16
RING = 4
NT = (((1,), (1,)), ((), ()))
TN = (((0,), (0,)), ((), ()))


def lanes(values):
    return jnp.concatenate(values, axis=1)


def sums_kernel(order, cols, x_ref, w_ref, hidden_ref, gate_delta_ref, up_delta_ref, acc):
    step = pl.program_id(0)
    tok_rows = hidden_ref.shape[1]

    @pl.when(step == 0)
    def _():
        acc[...] = jnp.zeros_like(acc)

    for i in range(4):
        owner = order[step] * 2 + i // 2
        feat = x_ref[0, :tok_rows, i * BLK : (i + 1) * BLK]
        cot = x_ref[0, tok_rows:, i * BLK : (i + 1) * BLK]
        for t in range(3):
            left = cot if t == 2 else feat
            for pair in range(0, NZ, 2):
                row = (t * 2 + i % 2) * NZ * BLK + pair * BLK
                right = lanes(
                    [w_ref[i // 2, row : row + BLK, :], w_ref[i // 2, row + BLK : row + 2 * BLK, :]]
                )
                prod = jnp.dot(left, right, preferred_element_type=jnp.float32)
                for h in range(2):
                    col = cols[owner * 24 + t * 8 + (i % 2) * NZ + pair + h]
                    acc[t, col] += prod[:, h * BLK : (h + 1) * BLK]

    @pl.when(step == pl.num_programs(0) - 1)
    def _():
        @pl.loop(0, FB_DEV)
        def _(f):
            gate = acc[0, f]
            up = acc[1, f]
            grad = acc[2, f]
            sig = jax.nn.sigmoid(gate)
            silu = gate * sig
            hidden_ref[f] = (silu * up).astype(jnp.bfloat16)
            up_delta_ref[f] = (grad * silu).astype(jnp.bfloat16)
            gate_delta_ref[f] = (grad * up * sig * (1.0 + gate * (1.0 - sig))).astype(jnp.bfloat16)


def weight_grads_kernel(scale, count, at_x, owners, cols, x_ref, *refs):
    hidden_ref, gate_delta_ref, up_delta_ref = refs[:3]
    step = pl.program_id(0)
    owner = owners[step]
    tok_rows = hidden_ref.shape[1]
    for i in range(2):
        at = pl.ds(pl.multiple_of((owner % 2) * 2 * BLK + i * BLK, BLK), BLK)
        feat = x_ref[0, :tok_rows, at]
        cot = x_ref[0, tok_rows:, at]
        for t, source in enumerate((gate_delta_ref, up_delta_ref, hidden_ref)):
            left = cot if t == 2 else feat
            base = owner * 24 + t * 8 + i * NZ
            right = lanes([source[cols[base + s]] for s in range(NZ)])
            prod = lax.dot_general(left, right, TN, preferred_element_type=jnp.float32) * scale
            for s in range(NZ):
                row = (t * 2 + i) * NZ * BLK + s * BLK
                value = prod[:, s * BLK : (s + 1) * BLK]
                if count:
                    got = refs[3][0, row : row + BLK, :].astype(jnp.float32)
                    value = value + got
                    held = refs[4 + count]
                    held[step, row : row + BLK, :] = value.astype(jnp.bfloat16)
                else:
                    refs[-1][0, row : row + BLK, :] = value.astype(jnp.bfloat16)
    if count:
        outs, held, sems = refs[4 : 4 + count], refs[4 + count], refs[5 + count]
        for n in range(count):

            @pl.when(step == n)
            def _():
                pltpu.make_async_copy(held.at[n], outs[n], sems.at[n]).start()

        @pl.when(step == count - 1)
        def _():
            for n in range(count):
                pltpu.make_async_copy(held.at[n], outs[n], sems.at[n]).wait()


def product_kernel(tensors, flip, cols, w_ref, *refs):
    step = pl.program_id(0)
    sources, o_ref = refs[:-1], refs[-1]
    for i in range(4):
        owner = step * 2 + i // 2
        left, right = [], []
        for n, t in enumerate(tensors):
            base = owner * 24 + t * 8 + (i % 2) * NZ
            row = (n * 2 + i % 2) * NZ * BLK
            for s in range(NZ):
                left.append(sources[n][cols[base + s]])
                right.append(w_ref[i // 2, row + s * BLK : row + (s + 1) * BLK, :])
        prod = lax.dot_general(lanes(left), lanes(right), NT, preferred_element_type=jnp.float32)
        o_ref[0, :, i * BLK : (i + 1) * BLK] = prod.astype(jnp.bfloat16)


def cost(flops, moved):
    return pl.CostEstimate(flops=flops, bytes_accessed=moved, transcendentals=0)


def params(megabytes):
    return pltpu.CompilerParams(
        dimension_semantics=("arbitrary",), vmem_limit_bytes=megabytes * 1024 * 1024
    )


def whole(shape):
    return pl.BlockSpec(shape, lambda j, *_: (0,) * len(shape))


def local_sums(order, cols, feats, weights):
    steps, rows2, width = feats.shape
    tok_rows = rows2 // 2
    shape = (FB_DEV, tok_rows, BLK)
    per = weights.shape[1]
    out = jax.ShapeDtypeStruct(shape, jnp.bfloat16)
    return pl.pallas_call(
        sums_kernel,
        out_shape=(out, out, out),
        grid_spec=pltpu.PrefetchScalarGridSpec(
            num_scalar_prefetch=2,
            grid=(steps,),
            in_specs=[
                pl.BlockSpec((1, rows2, width), lambda j, order, cols: (j, 0, 0)),
                pl.BlockSpec((2, per, BLK), lambda j, order, cols: (order[j], 0, 0)),
            ],
            out_specs=[whole(shape)] * 3,
            scratch_shapes=[pltpu.VMEM((3,) + shape, jnp.float32)],
        ),
        compiler_params=params(56),
        cost_estimate=cost(10**10, 30 * 10**6),
        name="local_sums",
    )(order, cols, feats, weights)


def weight_grads(at_x, owners, cols, feats, sources, scale, got=None):
    _, rows2, width = feats.shape
    count = owners.shape[0]
    rows = 3 * 2 * NZ * BLK
    block = pl.BlockSpec((1, rows, BLK), lambda j, *_: (j, 0, 0))
    in_specs = [pl.BlockSpec((1, rows2, width), lambda j, at_x, *_: (at_x[j], 0, 0))]
    in_specs += [pl.BlockSpec(memory_space=pltpu.VMEM)] * 3
    if got is None:
        out_shape = jax.ShapeDtypeStruct((count, rows, BLK), jnp.bfloat16)
        out_specs, scratch, extra = block, [], ()
    else:
        in_specs.append(block)
        out_shape = (jax.ShapeDtypeStruct((rows, BLK), jnp.bfloat16),) * count
        out_specs = (pl.BlockSpec(memory_space=pl.ANY),) * count
        scratch = [
            pltpu.VMEM((count, rows, BLK), jnp.bfloat16),
            pltpu.SemaphoreType.DMA((count,)),
        ]
        extra = (got,)
    return pl.pallas_call(
        functools.partial(weight_grads_kernel, scale, 0 if got is None else count),
        out_shape=out_shape,
        grid_spec=pltpu.PrefetchScalarGridSpec(
            num_scalar_prefetch=3,
            grid=(count,),
            in_specs=in_specs,
            out_specs=out_specs,
            scratch_shapes=scratch,
        ),
        compiler_params=params(28),
        cost_estimate=cost(count * 10**9, count * 3 * 10**6),
        name="weight_grads",
    )(at_x, owners, cols, feats, *sources, *extra)


def block_product(tensors, flip, cols, weights, sources):
    tok_rows = sources[0].shape[1]
    steps = weights.shape[0] // 2
    rows = len(tensors) * 2 * NZ * BLK
    at = tensors[0] * 2 * NZ * BLK // rows
    return pl.pallas_call(
        functools.partial(product_kernel, tensors),
        out_shape=jax.ShapeDtypeStruct((steps, tok_rows, 4 * BLK), jnp.bfloat16),
        grid_spec=pltpu.PrefetchScalarGridSpec(
            num_scalar_prefetch=2,
            grid=(steps,),
            in_specs=[pl.BlockSpec((2, rows, BLK), lambda j, flip, cols: (j, at, 0))]
            + [whole(sources[0].shape)] * len(sources),
            out_specs=pl.BlockSpec(
                (1, tok_rows, 4 * BLK), lambda j, flip, cols: (j // 2 * 2 + (j + flip[0]) % 2, 0, 0)
            ),
        ),
        compiler_params=params(40),
        cost_estimate=cost(len(tensors) * 3 * 10**9, len(tensors) * 7 * 10**6),
        name="block_product",
    )(flip, cols, weights, *sources)


def permute(value, axis, target):
    return lax.ppermute(value, axis, [(i, target(i)) for i in range(lax.axis_size(axis))])


def over_x(value, shift):
    return permute(value, "col", lambda c: ((c // 2 + shift) % RING) * 2 + c % 2)


def over_y(value, shift):
    return permute(value, "row", lambda r: ((r // 4 + shift) % RING) * 4 + r % 4)


def gather_features(own):
    x, z = lax.axis_index("col") // 2, lax.axis_index("col") % 2
    near = permute(own, "col", lambda c: c ^ 1)
    own_m, own_p = over_x(own, 1), over_x(own, -1)
    near_m, near_p = over_x(near, 1), over_x(near, -1)
    own_far, near_far = over_x(own_m, 1), over_x(near_p, -1)
    pieces = [own, near, own_p, near_p, own_far, near_far, own_m, near_m]
    order = [((x + n // 2) % RING) * 2 + (z + n) % 2 for n in range(8)]
    return jnp.stack(pieces), jnp.stack(order).astype(jnp.int32)


def slot_tables(shifts, half):
    x, z = lax.axis_index("col") // 2, lax.axis_index("col") % 2
    row = lax.axis_index("row")
    chips = [((row // 4 + d) % RING, (row // 2 + e) % 2) for d, e in shifts]
    at_x = [((y - x) % RING) * 2 + (h - z) % 2 for y, h in chips]
    owners = [y * 4 + h * 2 + (row + half) % 2 for y, h in chips]
    return jnp.stack(at_x).astype(jnp.int32), jnp.stack(owners).astype(jnp.int32)


FAR = ((2, 0), (2, 1))
NEAR = ((1, 1), (-1, 1), (1, 0), (-1, 0))
OWN = ((0, 0), (0, 1))


def body(tokens, cotangent, gate_blocks, up_blocks, down_blocks, gate_cols, up_cols, down_cols):
    n_row = lax.axis_size("row")
    tok_rows = tokens.shape[0]
    tables = jnp.concatenate([t.reshape(1, -1) for t in (gate_cols, up_cols, down_cols)], 1)
    tables = jnp.bitwise_and(tables, FB_DEV - 1).astype(jnp.bfloat16)
    tables = jnp.pad(tables, ((0, 15), (0, BLK - tables.shape[1])))
    packed = jnp.concatenate(
        [b.reshape(-1, BLK) for b in (gate_blocks, up_blocks, down_blocks)] + [tables], 0
    )
    weights = lax.all_gather(packed, "row", axis=0, tiled=True).reshape(n_row, -1, BLK)
    feats, order = gather_features(jnp.concatenate([tokens, cotangent], 0))
    at = packed.shape[0] - 16
    cols = weights[:, at, : 3 * 2 * NZ].astype(jnp.int32).reshape(-1)
    hidden, gate_delta, up_delta = local_sums(order, cols, feats, weights)
    sources = (hidden, gate_delta, up_delta)
    scale = float(tok_rows * n_row) ** (-0.5)

    def after(value):
        return lax.optimization_barrier((cols, value))[0]

    def theirs(shifts, cols):
        return weight_grads(*slot_tables(shifts, 1), cols, feats, sources, scale)

    def mine(shifts, cols, got):
        return weight_grads(*slot_tables(shifts, 0), cols, feats, sources, scale, got)

    def other_core(value):
        return permute(value, "row", lambda r: r ^ 1)

    def total(*values):
        return sum(v.astype(jnp.float32) for v in values).astype(jnp.bfloat16)

    rings = [[2 * x + z for x in range(RING)] for z in range(2)]

    def reduce_features(parts):
        ring_sum = lax.psum_scatter(
            parts.reshape(-1, parts.shape[2]), "col", scatter_dimension=0, tiled=True,
            axis_index_groups=rings,
        )
        got = permute(ring_sum[tok_rows:], "col", lambda c: c ^ 1)
        return total(ring_sum[:tok_rows], got)

    flip = (lax.axis_index("col") % 2).astype(jnp.int32).reshape(1)
    out_parts = block_product((2,), flip, cols, weights, (hidden,))
    output = reduce_features(out_parts)
    their_far = theirs(FAR, after(out_parts))
    got_far = other_core(their_far)
    their_near = theirs(NEAR, after(their_far))
    got_near = other_core(their_near)
    far0, far1 = mine(FAR, after(their_near), got_far)
    far_p, far_m = over_y(far0, 1), over_y(far1, -1)
    in_parts = block_product((0, 1), flip, after(far0), weights, (gate_delta, up_delta))
    tokens_grad = reduce_features(in_parts)
    their_own = theirs(OWN, after(in_parts))
    got_own = other_core(their_own)
    p1, m1, p0, m0 = mine(NEAR, after(their_own), got_near)
    from_m1, from_p1 = over_y(p1, 1), over_y(total(m1, far_m), -1)
    from_m0, from_p0 = over_y(total(p0, far_p), 1), over_y(m0, -1)
    own0, own1 = mine(OWN, after(p1), got_own)
    last = permute(total(own1, from_m1, from_p1), "row", lambda r: r ^ 2)
    grads = total(own0, from_m0, from_p0, last)
    gate_grad, up_grad, down_grad = (
        g.reshape(gate_blocks.shape) for g in jnp.split(grads, 3, axis=0)
    )
    return (output, tokens_grad, gate_grad, up_grad, down_grad)


def solution(mesh):
    flat, blocks = P("row", "col"), P("row", "col", None, None)
    in_specs = (flat, flat, blocks, blocks, blocks, flat, flat, flat)
    out_specs = (flat, flat, blocks, blocks, blocks)
    return jax.shard_map(body, mesh=mesh, in_specs=in_specs, out_specs=out_specs, check_vma=False)
```

```python
import functools

import jax
import jax.numpy as jnp
from jax import lax
from jax.experimental import pallas as pl
from jax.experimental.pallas import tpu as pltpu
from jax.sharding import PartitionSpec as P

BLK = 128
NZ = 4
FB_DEV = 16
RING = 4
NT = (((1,), (1,)), ((), ()))
TN = (((0,), (0,)), ((), ()))


def lanes(values):
    return jnp.concatenate(values, axis=1)


def sums_kernel(order, cols, x_ref, w_ref, hidden_ref, gate_delta_ref, up_delta_ref, acc):
    step = pl.program_id(0)
    tok_rows = hidden_ref.shape[1]

    @pl.when(step == 0)
    def _():
        acc[...] = jnp.zeros_like(acc)

    for i in range(4):
        owner = order[step] * 2 + i // 2
        feat = x_ref[0, :tok_rows, i * BLK : (i + 1) * BLK]
        cot = x_ref[0, tok_rows:, i * BLK : (i + 1) * BLK]
        for t in range(3):
            left = cot if t == 2 else feat
            for pair in range(0, NZ, 2):
                row = (t * 2 + i % 2) * NZ * BLK + pair * BLK
                right = lanes(
                    [w_ref[i // 2, row : row + BLK, :], w_ref[i // 2, row + BLK : row + 2 * BLK, :]]
                )
                prod = jnp.dot(left, right, preferred_element_type=jnp.float32)
                for h in range(2):
                    col = cols[owner * 24 + t * 8 + (i % 2) * NZ + pair + h]
                    acc[t, col] += prod[:, h * BLK : (h + 1) * BLK]

    @pl.when(step == pl.num_programs(0) - 1)
    def _():
        @pl.loop(0, FB_DEV)
        def _(f):
            gate = acc[0, f]
            up = acc[1, f]
            grad = acc[2, f]
            sig = jax.nn.sigmoid(gate)
            silu = gate * sig
            hidden_ref[f] = (silu * up).astype(jnp.bfloat16)
            up_delta_ref[f] = (grad * silu).astype(jnp.bfloat16)
            gate_delta_ref[f] = (grad * up * sig * (1.0 + gate * (1.0 - sig))).astype(jnp.bfloat16)


def weight_grads_kernel(scale, count, at_x, owners, cols, x_ref, *refs):
    hidden_ref, gate_delta_ref, up_delta_ref = refs[:3]
    step = pl.program_id(0)
    owner = owners[step]
    tok_rows = hidden_ref.shape[1]
    for i in range(2):
        at = pl.ds(pl.multiple_of((owner % 2) * 2 * BLK + i * BLK, BLK), BLK)
        feat = x_ref[0, :tok_rows, at]
        cot = x_ref[0, tok_rows:, at]
        for t, source in enumerate((gate_delta_ref, up_delta_ref, hidden_ref)):
            left = cot if t == 2 else feat
            base = owner * 24 + t * 8 + i * NZ
            right = lanes([source[cols[base + s]] for s in range(NZ)])
            prod = lax.dot_general(left, right, TN, preferred_element_type=jnp.float32) * scale
            for s in range(NZ):
                row = (t * 2 + i) * NZ * BLK + s * BLK
                value = prod[:, s * BLK : (s + 1) * BLK]
                if count:
                    got = refs[3][0, row : row + BLK, :].astype(jnp.float32)
                    value = value + got
                    held = refs[4 + count]
                    held[step, row : row + BLK, :] = value.astype(jnp.bfloat16)
                else:
                    refs[-1][0, row : row + BLK, :] = value.astype(jnp.bfloat16)
    if count:
        outs, held, sems = refs[4 : 4 + count], refs[4 + count], refs[5 + count]
        for n in range(count):

            @pl.when(step == n)
            def _():
                pltpu.make_async_copy(held.at[n], outs[n], sems.at[n]).start()

        @pl.when(step == count - 1)
        def _():
            for n in range(count):
                pltpu.make_async_copy(held.at[n], outs[n], sems.at[n]).wait()


def product_kernel(tensors, flip, cols, w_ref, *refs):
    step = pl.program_id(0)
    sources, o_ref = refs[:-1], refs[-1]
    for i in range(4):
        owner = step * 2 + i // 2
        left, right = [], []
        for n, t in enumerate(tensors):
            base = owner * 24 + t * 8 + (i % 2) * NZ
            row = (n * 2 + i % 2) * NZ * BLK
            for s in range(NZ):
                left.append(sources[n][cols[base + s]])
                right.append(w_ref[i // 2, row + s * BLK : row + (s + 1) * BLK, :])
        prod = lax.dot_general(lanes(left), lanes(right), NT, preferred_element_type=jnp.float32)
        o_ref[0, :, i * BLK : (i + 1) * BLK] = prod.astype(jnp.bfloat16)


def cost(flops, moved):
    return pl.CostEstimate(flops=flops, bytes_accessed=moved, transcendentals=0)


def params(megabytes):
    return pltpu.CompilerParams(
        dimension_semantics=("arbitrary",), vmem_limit_bytes=megabytes * 1024 * 1024
    )


def whole(shape):
    return pl.BlockSpec(shape, lambda j, *_: (0,) * len(shape))


def local_sums(order, cols, feats, weights):
    steps, rows2, width = feats.shape
    tok_rows = rows2 // 2
    shape = (FB_DEV, tok_rows, BLK)
    per = weights.shape[1]
    out = jax.ShapeDtypeStruct(shape, jnp.bfloat16)
    return pl.pallas_call(
        sums_kernel,
        out_shape=(out, out, out),
        grid_spec=pltpu.PrefetchScalarGridSpec(
            num_scalar_prefetch=2,
            grid=(steps,),
            in_specs=[
                pl.BlockSpec((1, rows2, width), lambda j, order, cols: (j, 0, 0)),
                pl.BlockSpec((2, per, BLK), lambda j, order, cols: (order[j], 0, 0)),
            ],
            out_specs=[whole(shape)] * 3,
            scratch_shapes=[pltpu.VMEM((3,) + shape, jnp.float32)],
        ),
        compiler_params=params(56),
        cost_estimate=cost(10**10, 30 * 10**6),
        name="local_sums",
    )(order, cols, feats, weights)


def weight_grads(at_x, owners, cols, feats, sources, scale, got=None):
    _, rows2, width = feats.shape
    count = owners.shape[0]
    rows = 3 * 2 * NZ * BLK
    block = pl.BlockSpec((1, rows, BLK), lambda j, *_: (j, 0, 0))
    in_specs = [pl.BlockSpec((1, rows2, width), lambda j, at_x, *_: (at_x[j], 0, 0))]
    in_specs += [pl.BlockSpec(memory_space=pltpu.VMEM)] * 3
    if got is None:
        out_shape = jax.ShapeDtypeStruct((count, rows, BLK), jnp.bfloat16)
        out_specs, scratch, extra = block, [], ()
    else:
        in_specs.append(block)
        out_shape = (jax.ShapeDtypeStruct((rows, BLK), jnp.bfloat16),) * count
        out_specs = (pl.BlockSpec(memory_space=pl.ANY),) * count
        scratch = [
            pltpu.VMEM((count, rows, BLK), jnp.bfloat16),
            pltpu.SemaphoreType.DMA((count,)),
        ]
        extra = (got,)
    return pl.pallas_call(
        functools.partial(weight_grads_kernel, scale, 0 if got is None else count),
        out_shape=out_shape,
        grid_spec=pltpu.PrefetchScalarGridSpec(
            num_scalar_prefetch=3,
            grid=(count,),
            in_specs=in_specs,
            out_specs=out_specs,
            scratch_shapes=scratch,
        ),
        compiler_params=params(28),
        cost_estimate=cost(count * 10**9, count * 3 * 10**6),
        name="weight_grads",
    )(at_x, owners, cols, feats, *sources, *extra)


def block_product(tensors, flip, cols, weights, sources):
    tok_rows = sources[0].shape[1]
    steps = weights.shape[0] // 2
    rows = len(tensors) * 2 * NZ * BLK
    at = tensors[0] * 2 * NZ * BLK // rows
    return pl.pallas_call(
        functools.partial(product_kernel, tensors),
        out_shape=jax.ShapeDtypeStruct((steps, tok_rows, 4 * BLK), jnp.bfloat16),
        grid_spec=pltpu.PrefetchScalarGridSpec(
            num_scalar_prefetch=2,
            grid=(steps,),
            in_specs=[pl.BlockSpec((2, rows, BLK), lambda j, flip, cols: (j, at, 0))]
            + [whole(sources[0].shape)] * len(sources),
            out_specs=pl.BlockSpec(
                (1, tok_rows, 4 * BLK), lambda j, flip, cols: (j // 2 * 2 + (j + flip[0]) % 2, 0, 0)
            ),
        ),
        compiler_params=params(40),
        cost_estimate=cost(len(tensors) * 3 * 10**9, len(tensors) * 7 * 10**6),
        name="block_product",
    )(flip, cols, weights, *sources)


def permute(value, axis, target):
    return lax.ppermute(value, axis, [(i, target(i)) for i in range(lax.axis_size(axis))])


def over_x(value, shift):
    return permute(value, "col", lambda c: ((c // 2 + shift) % RING) * 2 + c % 2)


def over_y(value, shift):
    return permute(value, "row", lambda r: ((r // 4 + shift) % RING) * 4 + r % 4)


def gather_features(own):
    x, z = lax.axis_index("col") // 2, lax.axis_index("col") % 2
    near = permute(own, "col", lambda c: c ^ 1)
    own_m, own_p = over_x(own, 1), over_x(own, -1)
    near_m, near_p = over_x(near, 1), over_x(near, -1)
    own_far, near_far = over_x(own_m, 1), over_x(near_p, -1)
    pieces = [own, near, own_p, near_p, own_far, near_far, own_m, near_m]
    order = [((x + n // 2) % RING) * 2 + (z + n) % 2 for n in range(8)]
    return jnp.stack(pieces), jnp.stack(order).astype(jnp.int32)


def slot_tables(shifts, half):
    x, z = lax.axis_index("col") // 2, lax.axis_index("col") % 2
    row = lax.axis_index("row")
    chips = [((row // 4 + d) % RING, (row // 2 + e) % 2) for d, e in shifts]
    at_x = [((y - x) % RING) * 2 + (h - z) % 2 for y, h in chips]
    owners = [y * 4 + h * 2 + (row + half) % 2 for y, h in chips]
    return jnp.stack(at_x).astype(jnp.int32), jnp.stack(owners).astype(jnp.int32)


FAR = ((2, 0), (2, 1))
NEAR = ((1, 1), (-1, 1), (1, 0), (-1, 0))
OWN = ((0, 0), (0, 1))


def body(tokens, cotangent, gate_blocks, up_blocks, down_blocks, gate_cols, up_cols, down_cols):
    n_row = lax.axis_size("row")
    tok_rows = tokens.shape[0]
    tables = jnp.concatenate([t.reshape(1, -1) for t in (gate_cols, up_cols, down_cols)], 1)
    tables = jnp.bitwise_and(tables, FB_DEV - 1).astype(jnp.bfloat16)
    tables = jnp.pad(tables, ((0, 15), (0, BLK - tables.shape[1])))
    packed = jnp.concatenate(
        [b.reshape(-1, BLK) for b in (gate_blocks, up_blocks, down_blocks)] + [tables], 0
    )
    weights = lax.all_gather(packed, "row", axis=0, tiled=True).reshape(n_row, -1, BLK)
    feats, order = gather_features(jnp.concatenate([tokens, cotangent], 0))
    at = packed.shape[0] - 16
    cols = weights[:, at, : 3 * 2 * NZ].astype(jnp.int32).reshape(-1)
    hidden, gate_delta, up_delta = local_sums(order, cols, feats, weights)
    sources = (hidden, gate_delta, up_delta)
    scale = float(tok_rows * n_row) ** (-0.5)

    def after(value):
        return lax.optimization_barrier((cols, value))[0]

    def theirs(shifts, cols):
        return weight_grads(*slot_tables(shifts, 1), cols, feats, sources, scale)

    def mine(shifts, cols, got):
        return weight_grads(*slot_tables(shifts, 0), cols, feats, sources, scale, got)

    def other_core(value):
        return permute(value, "row", lambda r: r ^ 1)

    def total(*values):
        return sum(v.astype(jnp.float32) for v in values).astype(jnp.bfloat16)

    rings = [[2 * x + z for x in range(RING)] for z in range(2)]

    def reduce_features(parts):
        ring_sum = lax.psum_scatter(
            parts.reshape(-1, parts.shape[2]), "col", scatter_dimension=0, tiled=True,
            axis_index_groups=rings,
        )
        got = permute(ring_sum[tok_rows:], "col", lambda c: c ^ 1)
        return total(ring_sum[:tok_rows], got)

    flip = (lax.axis_index("col") % 2).astype(jnp.int32).reshape(1)
    their_far = theirs(FAR, cols)
    got_far = other_core(their_far)
    out_parts = block_product((2,), flip, after(their_far), weights, (hidden,))
    output = reduce_features(out_parts)
    far0, far1 = mine(FAR, after(out_parts), got_far)
    far_p, far_m = over_y(far0, 1), over_y(far1, -1)
    their_near = theirs(NEAR, after(far0))
    got_near = other_core(their_near)
    their_own = theirs(OWN, after(their_near))
    got_own = other_core(their_own)
    p1, m1, p0, m0 = mine(NEAR, after(their_own), got_near)
    m1, p0 = total(m1, far_m), total(p0, far_p)
    from_m1, from_p1 = over_y(p1, 1), over_y(m1, -1)
    from_m0, from_p0 = over_y(p0, 1), over_y(m0, -1)
    ready = lax.optimization_barrier((cols, p1, m1, p0))[0]
    in_parts = block_product((0, 1), flip, ready, weights, (gate_delta, up_delta))
    tokens_grad = reduce_features(in_parts)
    own0, own1 = mine(OWN, lax.optimization_barrier((cols, in_parts, output))[0], got_own)
    last = permute(total(own1, from_m1, from_p1), "row", lambda r: r ^ 2)
    grads = total(own0, from_m0, from_p0, last)
    gate_grad, up_grad, down_grad = (
        g.reshape(gate_blocks.shape) for g in jnp.split(grads, 3, axis=0)
    )
    return (output, tokens_grad, gate_grad, up_grad, down_grad)


def solution(mesh):
    flat, blocks = P("row", "col"), P("row", "col", None, None)
    in_specs = (flat, flat, blocks, blocks, blocks, flat, flat, flat)
    out_specs = (flat, flat, blocks, blocks, blocks)
    return jax.shard_map(body, mesh=mesh, in_specs=in_specs, out_specs=out_specs, check_vma=False)
```
